32 devices in a mesh: atoms: 4 (over y, x), energy: 8 (over z, core).
Axes of the slice: x: 2, y: 2, z: 4, core: 2. Of those that a mesh axis runs over, the one named last changes fastest.
Arguments:
- retarded_green_blocks: bfloat16 [4, 24, 2, 384, 384], P('atoms', 'energy'), may hold values from -0.21875 to 0.21875
- contact_lesser_sigma: bfloat16 [4, 24, 2, 384, 384], P('atoms', 'energy'), may hold values from -6 to 6
- energy_counts: int32 [8], replicated, may hold values from 1 to 3, 15 in all
- phonon_shift: int32 [64], replicated, may hold values from 1 to 7
- phonon_weight: float32 [4, 64], replicated, may hold values from 0.01 to 0.1
Outputs:
- scattered: bfloat16 [4, 24, 2, 384, 384], P('atoms', 'energy')
The draws below stay inside these ranges and needn't reach their ends.
Inputs may be any that keep to these rules, and one draw needn't show every extreme that they name: energy_counts sums to 15; its largest entry is exactly 3.
All inputs are finite; a program needn't handle non-finite values.
Results may differ from the reference program's by a relative error of at most 0.007.
Values may be sent and summed in bfloat16 or wider, within the bound.
A program may use at most 64 MiB of HBM per device.

```python
import math
import jax
import jax.numpy as jnp
import numpy as np
from jax import lax

BLOCK_ORBITALS = 384
NW = 64
NE_DEV = 3
ENERGY_SLOTS = 24
TOTAL = 15
SLAB_BLOCKS = 4
N_ENERGY = 8


def place_ends(values, stream_key, smallest, largest):
    longest = values.shape.index(max(values.shape))
    spots = []
    for shift in (0, 1):
        where = [jax.random.randint(jax.random.fold_in(stream_key, axis), (), 0, length) for axis, length in enumerate(values.shape)]
        where[longest] = (where[longest] + shift) % values.shape[longest]
        spots.append(tuple(where))
    return values.at[spots[0]].set(smallest).at[spots[1]].set(largest)


def levels(stream_key, shape, split, least, top_value):
    factor_of, own = 1.0, jax.random.fold_in(stream_key, 6)
    for position, shards_of in split:
        draws = jnp.exp(jax.random.uniform(jax.random.fold_in(own, position), (shards_of,), jnp.float32, least / len(split), top_value / len(split)))
        factor_of = factor_of * jnp.repeat(draws, shape[position] // shards_of).reshape([-1 if axis == position else 1 for axis in range(len(shape))])
    return factor_of


def profile(amount, total, most, lean):
    loads = [(1 << 20) // math.isqrt(standing ** lean) + 1 for standing in range(2, amount + 1)]
    spare, given = total - most - (amount - 1), [1] * (amount - 1)
    while spare > 0:
        candidates = [i for i in range(amount - 1) if given[i] < most]
        whole, remaining = sum([loads[i] for i in candidates]), spare
        for i in candidates:
            more = min(most - given[i], max(1, remaining * loads[i] // whole), spare)
            given[i] = given[i] + more
            spare = spare - more
    return np.array([most] + given)


def uneven_parts(key, number_of, total, bound, skew):
    if number_of == 2:
        one = jax.random.randint(key, (), max(1, total - bound), min(bound, total - 1) + 1)
        return jnp.stack([one, total - one])
    sizes = jnp.asarray(profile(number_of, total, bound, skew), jnp.int32)
    pairs = (number_of - 1) // 2
    source_of, taker = sizes[1:1 + 2 * pairs:2], sizes[2:2 + 2 * pairs:2]
    slack = jnp.minimum(source_of - 1, bound - taker)
    shifted = jax.random.randint(jax.random.fold_in(key, 1), (pairs,), 0, 1 << 20) % (slack + 1)
    sizes = sizes.at[1:1 + 2 * pairs:2].set(source_of - shifted).at[2:2 + 2 * pairs:2].set(taker + shifted)
    return sizes[jax.random.permutation(jax.random.fold_in(key, 2), number_of)]


def bell_draw(own_key, extent, deviation, bound, pieces=(), kind=jnp.bfloat16):
    result = jax.random.normal(own_key, extent, jnp.float32) * deviation
    if len(pieces) > 0:
        result = levels(own_key, extent, pieces, -0.22, 0.18) * result
    return jnp.clip(result, min=-bound, max=bound).astype(kind)


def setup_inputs(seed: int = 0) -> dict:
    key_of = jax.random.split(jax.random.key(seed), 6)
    retarded_green_blocks = bell_draw(key_of[0], (SLAB_BLOCKS, ENERGY_SLOTS, 2, BLOCK_ORBITALS, BLOCK_ORBITALS), (2 * BLOCK_ORBITALS) ** -0.5, 0.21875, ((0, 4), (1, 8)))
    contact_lesser_sigma = bell_draw(key_of[1], (SLAB_BLOCKS, ENERGY_SLOTS, 2, BLOCK_ORBITALS, BLOCK_ORBITALS), 1.0, 6.0, ((0, 4), (1, 8)))
    energy_counts = uneven_parts(key_of[2], N_ENERGY, TOTAL, NE_DEV, 1).astype(jnp.int32)
    phonon_shift = place_ends(jax.random.randint(key_of[3], (NW,), 1, TOTAL // 2 + 1), jax.random.fold_in(key_of[3], 1), 1, (TOTAL // 2 + 1) - 1).astype(jnp.int32)
    phonon_weight = jnp.clip(jnp.exp(jax.random.uniform(key_of[4], (4, NW), jnp.float32, math.log(0.01), math.log(0.1))), 0.01, 0.1)
    return dict(retarded_green_blocks=retarded_green_blocks, contact_lesser_sigma=contact_lesser_sigma, energy_counts=energy_counts, phonon_shift=phonon_shift, phonon_weight=phonon_weight)


def complex_product(left, right):
    prods = jnp.einsum("spik,sqkj->spqij", left.astype(jnp.float32), right.astype(jnp.float32))
    return jnp.stack([prods[:, 0, 0] - prods[:, 1, 1], prods[:, 0, 1] + prods[:, 1, 0]], axis=1)


def product_adjoint(left, right):
    prods = jnp.einsum("spik,sqjk->spqij", left.astype(jnp.float32), right.astype(jnp.float32))
    return jnp.stack([prods[:, 0, 0] + prods[:, 1, 1], prods[:, 1, 0] - prods[:, 0, 1]], axis=1)


def kernels(energy_counts, phonon_shift, phonon_weight, groups, per_group):
    total_slots = groups * per_group
    starts = (jnp.cumsum(energy_counts) - energy_counts).astype(jnp.int32)
    slot_numbers = jnp.arange(total_slots, dtype=jnp.int32)
    owner = slot_numbers // per_group
    within = slot_numbers % per_group
    energy_index = starts[owner] + within
    live = (within < energy_counts[owner]).astype(jnp.float32)
    spacing = energy_index[None, :] - energy_index[:, None]
    upward = (spacing[:, :, None] == phonon_shift[None, None, :]).astype(jnp.float32)
    downward = (spacing[:, :, None] == -phonon_shift[None, None, :]).astype(jnp.float32)
    mask = live[:, None] * live[None, :]
    own_kernel = jnp.sum(upward * phonon_weight[0] + downward * phonon_weight[1], axis=-1) * mask
    side_kernel = jnp.sum(upward * phonon_weight[2] + downward * phonon_weight[3], axis=-1) * mask
    return own_kernel.astype(jnp.bfloat16), side_kernel.astype(jnp.bfloat16)


def reference(retarded_green_blocks, contact_lesser_sigma, energy_counts, phonon_shift, phonon_weight):
    own_kernel, side_kernel = kernels(energy_counts, phonon_shift, phonon_weight, N_ENERGY, NE_DEV)

    def dyson(pair):
        retarded, lesser_in = pair
        mixed = complex_product(retarded, lesser_in).astype(jnp.bfloat16)
        return product_adjoint(mixed, retarded).astype(jnp.bfloat16)

    lesser = lax.map(dyson, (retarded_green_blocks, contact_lesser_sigma))
    blank = jnp.zeros_like(lesser[:1])
    padded = jnp.concatenate([blank, lesser, blank], axis=0)
    own_f = own_kernel.astype(jnp.float32)
    side_f = side_kernel.astype(jnp.float32)

    def per_block(index):
        below = lax.dynamic_index_in_dim(padded, index, 0, keepdims=False).astype(jnp.float32)
        middle_block = lax.dynamic_index_in_dim(padded, index + 1, 0, keepdims=False).astype(jnp.float32)
        above = lax.dynamic_index_in_dim(padded, index + 2, 0, keepdims=False).astype(jnp.float32)
        sigma = jnp.einsum("jk,kpab->jpab", own_f, middle_block)
        sigma = sigma + jnp.einsum("jk,kpab->jpab", side_f, below) + jnp.einsum("jk,kpab->jpab", side_f, above)
        sigma = sigma.astype(jnp.bfloat16)
        retarded = lax.dynamic_index_in_dim(retarded_green_blocks, index, 0, keepdims=False)
        return complex_product(retarded, sigma).astype(jnp.bfloat16)

    return lax.map(per_block, jnp.arange(retarded_green_blocks.shape[0], dtype=jnp.int32))
```

```python
import functools

import jax
import jax.numpy as jnp
from jax import lax
from jax.experimental import pallas as pl
from jax.experimental.pallas import tpu as pltpu
from jax.sharding import PartitionSpec as P

TILE = 16
LANES = 128
MESH = pl.DeviceIdType.MESH


def coupling_tables(groups, per_group, counts_ref, shift_ref, weight_ref):
    rows = lax.broadcasted_iota(jnp.int32, (LANES, LANES), 0)
    lanes = lax.broadcasted_iota(jnp.int32, (LANES, LANES), 1)

    def slot_energy(index):
        energy = jnp.full((LANES, LANES), -1, jnp.int32)
        start = jnp.int32(0)
        for group in range(groups):
            count = counts_ref[group]
            for s in range(per_group):
                here = (index == group * per_group + s) & (s < count)
                energy = jnp.where(here, start + s, energy)
            start = start + count
        return energy

    energy_row = slot_energy(rows)
    energy_lane = slot_energy(lanes)
    own_space = energy_lane - energy_row
    side_space = energy_lane - rows

    def add(m, sums):
        own, side = sums
        shift = shift_ref[m]
        own = own + jnp.where(own_space == shift, weight_ref[0, m], 0.0)
        own = own + jnp.where(own_space == -shift, weight_ref[1, m], 0.0)
        side = side + jnp.where(side_space == shift, weight_ref[2, m], 0.0)
        side = side + jnp.where(side_space == -shift, weight_ref[3, m], 0.0)
        return own, side

    zero = jnp.zeros((LANES, LANES), jnp.float32)
    own, side = lax.fori_loop(0, shift_ref.shape[0], add, (zero, zero))
    own = jnp.where((energy_row >= 0) & (energy_lane >= 0), own, 0.0)
    side = jnp.where(energy_lane >= 0, side, 0.0)
    spread = jnp.where(energy_row == lanes, 1.0, 0.0)
    return own, side, spread


def spread_out(table, out_ref):
    height, width = out_ref.shape
    left_row = lax.broadcasted_iota(jnp.int32, (height, LANES), 0)
    left_lane = lax.broadcasted_iota(jnp.int32, (height, LANES), 1)
    left = jnp.where(left_row // TILE == left_lane, 1.0, 0.0).astype(jnp.bfloat16)
    right_row = lax.broadcasted_iota(jnp.int32, (LANES, width), 0)
    right_lane = lax.broadcasted_iota(jnp.int32, (LANES, width), 1)
    right = jnp.where(right_lane // TILE == right_row, 1.0, 0.0).astype(jnp.bfloat16)
    tall = jnp.dot(left, table.astype(jnp.bfloat16), preferred_element_type=jnp.float32)
    full = jnp.dot(tall.astype(jnp.bfloat16), right, preferred_element_type=jnp.float32)
    row = lax.broadcasted_iota(jnp.int32, (height, width), 0)
    lane = lax.broadcasted_iota(jnp.int32, (height, width), 1)
    out_ref[...] = jnp.where(row % TILE == lane % TILE, full, 0.0).astype(jnp.bfloat16)


def kernel(
    groups, blocks, counts_ref, shift_ref, weight_ref, r_ref, c_ref, o_ref,
    left, mixed, lesser, moved, own_mat, side_mat, spread_mat, side_part, below, above,
    sigma, back, total, send_a, recv_a, send_b, recv_b, local_a, local_b,
    send_up, recv_up, send_dn, recv_dn,
):
    per_group, _, orbitals, _ = r_ref.shape
    slots = groups * per_group
    chunks = moved.shape[0]
    depth = groups * TILE
    me = lax.axis_index("energy")
    block = lax.axis_index("atoms")
    has_below = block > 0
    has_above = block < blocks - 1

    barrier = pltpu.get_barrier_semaphore()
    for d in range(1, groups):
        pl.semaphore_signal(barrier, inc=1, device_id={"energy": lax.rem(me + d, groups)}, device_id_type=MESH)

    @pl.when(has_below)
    def _():
        pl.semaphore_signal(barrier, inc=1, device_id={"atoms": block - 1}, device_id_type=MESH)

    @pl.when(has_above)
    def _():
        pl.semaphore_signal(barrier, inc=1, device_id={"atoms": block + 1}, device_id_type=MESH)

    @pl.when(jnp.logical_not(has_below))
    def _():
        below[...] = jnp.zeros_like(below)

    @pl.when(jnp.logical_not(has_above))
    def _():
        above[...] = jnp.zeros_like(above)

    def complex_rows(dst, s, real, imag):
        dst[s, :orbitals, :orbitals] = real
        dst[s, :orbitals, orbitals:] = -imag
        dst[s, orbitals:, :orbitals] = imag
        dst[s, orbitals:, orbitals:] = real

    def mix(s, carry):
        complex_rows(left, s, r_ref[s, 0], r_ref[s, 1])
        contact = c_ref[s].reshape(2 * orbitals, orbitals)
        product = jnp.dot(left[s], contact, preferred_element_type=jnp.float32).astype(jnp.bfloat16)
        complex_rows(mixed, s, product[:orbitals], product[orbitals:])
        return carry

    lax.fori_loop(0, per_group, mix, 0)

    neighbours = jnp.where(has_below, 1, 0) + jnp.where(has_above, 1, 0)
    pl.semaphore_wait(barrier, groups - 1 + neighbours)

    def tile_rows(q, peer):
        return pl.ds(pl.multiple_of((q * groups + peer) * TILE, TILE), TILE)

    def out_copy(q, d):
        peer = lax.rem(me + d, groups)
        return pltpu.make_async_remote_copy(
            src_ref=lesser.at[:, tile_rows(q, peer), :],
            dst_ref=moved.at[q, pl.ds(me * per_group, per_group)],
            send_sem=send_a.at[q, d], recv_sem=recv_a.at[q, d],
            device_id={"energy": peer}, device_id_type=MESH,
        )

    def out_local(q):
        return pltpu.make_async_copy(
            lesser.at[:, tile_rows(q, me), :],
            moved.at[q, pl.ds(me * per_group, per_group)],
            local_a.at[q],
        )

    def back_copy(q, d):
        peer = lax.rem(me + d, groups)
        return pltpu.make_async_remote_copy(
            src_ref=sigma.at[q, pl.ds(peer * per_group, per_group)],
            dst_ref=back.at[:, tile_rows(q, me), :],
            send_sem=send_b.at[q, d], recv_sem=recv_b.at[q, d],
            device_id={"energy": peer}, device_id_type=MESH,
        )

    def back_local(q):
        return pltpu.make_async_copy(
            sigma.at[q, pl.ds(me * per_group, per_group)],
            back.at[:, tile_rows(q, me), :],
            local_b.at[q],
        )

    def up_copy(q):
        return pltpu.make_async_remote_copy(
            src_ref=side_part.at[q], dst_ref=below.at[q],
            send_sem=send_up.at[q], recv_sem=recv_up.at[q],
            device_id={"atoms": block + 1}, device_id_type=MESH,
        )

    def down_copy(q):
        return pltpu.make_async_remote_copy(
            src_ref=side_part.at[q], dst_ref=above.at[q],
            send_sem=send_dn.at[q], recv_sem=recv_dn.at[q],
            device_id={"atoms": block - 1}, device_id_type=MESH,
        )

    def send_lesser(q, carry):
        rows = pl.ds(pl.multiple_of(q * depth, depth), depth)
        for s in range(per_group):
            lesser[s, rows, :] = lax.dot_general(
                mixed[s, rows, :], left[s, :orbitals, :], (((1,), (1,)), ((), ())),
                preferred_element_type=jnp.float32,
            ).astype(jnp.bfloat16)
        for d in range(1, groups):
            out_copy(q, d).start()
        out_local(q).start()
        return carry

    lax.fori_loop(0, chunks, send_lesser, 0)

    own, side, spread = coupling_tables(groups, per_group, counts_ref, shift_ref, weight_ref)
    spread_out(own, own_mat)
    spread_out(side, side_mat)
    spread_out(spread, spread_mat)

    def send_side(q):
        for d in range(1, groups):
            out_copy(q, d).wait_recv()
        out_local(q).wait()
        values = moved[q].reshape(slots * TILE, orbitals)
        part = jnp.dot(side_mat[...], values, preferred_element_type=jnp.float32)
        side_part[q] = part.astype(jnp.bfloat16).reshape(side_part.shape[1:])

        @pl.when(has_above)
        def _():
            up_copy(q).start()

        @pl.when(has_below)
        def _():
            down_copy(q).start()

    def send_sigma(q):
        @pl.when(has_below)
        def _():
            up_copy(q).wait_recv()

        @pl.when(has_above)
        def _():
            down_copy(q).wait_recv()

        values = moved[q].reshape(slots * TILE, orbitals)
        flat = (side_mat.shape[0], orbitals)
        result = jnp.dot(own_mat[...], values, preferred_element_type=jnp.float32)
        result = result + jnp.dot(spread_mat[...], below[q].reshape(flat), preferred_element_type=jnp.float32)
        result = result + jnp.dot(spread_mat[...], above[q].reshape(flat), preferred_element_type=jnp.float32)
        sigma[q] = result.astype(jnp.bfloat16).reshape(sigma.shape[1:])
        for d in range(1, groups):
            back_copy(q, d).start()
        back_local(q).start()

    send_side(0)

    def middle(q, carry):
        send_side(q)
        send_sigma(q - 1)
        return carry

    lax.fori_loop(1, chunks, middle, 0)
    send_sigma(chunks - 1)

    def arrive(q, carry):
        for d in range(1, groups):
            back_copy(q, d).wait_recv()
        back_local(q).wait()
        return carry

    lax.fori_loop(0, chunks - 1, arrive, 0)
    cut = (chunks - 1) * depth

    def head(s, carry):
        total[s] = jnp.dot(left[s, :, :cut], back[s, :cut, :], preferred_element_type=jnp.float32)
        return carry

    lax.fori_loop(0, per_group, head, 0)
    arrive(chunks - 1, 0)

    def tail(s, carry):
        last = jnp.dot(left[s, :, cut:], back[s, cut:, :], preferred_element_type=jnp.float32)
        o_ref[s] = (total[s] + last).astype(jnp.bfloat16).reshape(2, orbitals, orbitals)
        return carry

    lax.fori_loop(0, per_group, tail, 0)

    def drain(q, carry):
        for d in range(1, groups):
            out_copy(q, d).wait_send()
            back_copy(q, d).wait_send()

        @pl.when(has_above)
        def _():
            up_copy(q).wait_send()

        @pl.when(has_below)
        def _():
            down_copy(q).wait_send()

        return carry

    lax.fori_loop(0, chunks, drain, 0)


def on_device(groups, blocks, retarded, contact, energy_counts, phonon_shift, phonon_weight):
    _, per_group, parts, orbitals, _ = retarded.shape
    slots = groups * per_group
    rows = parts * orbitals
    chunks = rows // (groups * TILE)
    energies = 2 * groups
    bf16, f32 = jnp.bfloat16, jnp.float32
    smem = pl.BlockSpec(memory_space=pltpu.SMEM)
    vmem = pl.BlockSpec(memory_space=pltpu.VMEM)
    dma = pltpu.SemaphoreType.DMA
    result = pl.pallas_call(
        functools.partial(kernel, groups, blocks),
        out_shape=jax.ShapeDtypeStruct(retarded.shape[1:], bf16),
        in_specs=[smem, smem, smem, vmem, vmem],
        out_specs=vmem,
        scratch_shapes=[
            pltpu.VMEM((per_group, rows, rows), bf16),
            pltpu.VMEM((per_group, rows, rows), bf16),
            pltpu.VMEM((per_group, rows, orbitals), bf16),
            pltpu.VMEM((chunks, slots, TILE, orbitals), bf16),
            pltpu.VMEM((slots * TILE, slots * TILE), bf16),
            pltpu.VMEM((energies * TILE, slots * TILE), bf16),
            pltpu.VMEM((slots * TILE, energies * TILE), bf16),
            pltpu.VMEM((chunks, energies, TILE, orbitals), bf16),
            pltpu.VMEM((chunks, energies, TILE, orbitals), bf16),
            pltpu.VMEM((chunks, energies, TILE, orbitals), bf16),
            pltpu.VMEM((chunks, slots, TILE, orbitals), bf16),
            pltpu.VMEM((per_group, rows, orbitals), bf16),
            pltpu.VMEM((per_group, rows, orbitals), f32),
            dma((chunks, groups)), dma((chunks, groups)),
            dma((chunks, groups)), dma((chunks, groups)),
            dma((chunks,)), dma((chunks,)),
            dma((chunks,)), dma((chunks,)), dma((chunks,)), dma((chunks,)),
        ],
        compiler_params=pltpu.CompilerParams(
            collective_id=0, has_side_effects=True, vmem_limit_bytes=60 << 20
        ),
    )(energy_counts, phonon_shift, phonon_weight, retarded[0], contact[0])
    return result[None]


def solution(mesh):
    split = P("atoms", "energy", None, None, None)
    return jax.shard_map(
        functools.partial(on_device, mesh.shape["energy"], mesh.shape["atoms"]),
        mesh=mesh, in_specs=(split, split, P(), P(), P()), out_specs=split, check_vma=False,
    )
```

```python
import functools

import jax
import jax.numpy as jnp
from jax import lax
from jax.experimental import pallas as pl
from jax.experimental.pallas import tpu as pltpu
from jax.sharding import PartitionSpec as P

TILE = 16
LANES = 128
MESH = pl.DeviceIdType.MESH


def coupling_tables(groups, per_group, counts_ref, shift_ref, weight_ref):
    rows = lax.broadcasted_iota(jnp.int32, (LANES, LANES), 0)
    lanes = lax.broadcasted_iota(jnp.int32, (LANES, LANES), 1)

    def slot_energy(index):
        energy = jnp.full((LANES, LANES), -1, jnp.int32)
        start = jnp.int32(0)
        for group in range(groups):
            count = counts_ref[group]
            for s in range(per_group):
                here = (index == group * per_group + s) & (s < count)
                energy = jnp.where(here, start + s, energy)
            start = start + count
        return energy

    energy_row = slot_energy(rows)
    energy_lane = slot_energy(lanes)
    own_space = energy_lane - energy_row
    side_space = energy_lane - rows

    def add(m, sums):
        own, side = sums
        shift = shift_ref[m]
        own = own + jnp.where(own_space == shift, weight_ref[0, m], 0.0)
        own = own + jnp.where(own_space == -shift, weight_ref[1, m], 0.0)
        side = side + jnp.where(side_space == shift, weight_ref[2, m], 0.0)
        side = side + jnp.where(side_space == -shift, weight_ref[3, m], 0.0)
        return own, side

    zero = jnp.zeros((LANES, LANES), jnp.float32)
    own, side = lax.fori_loop(0, shift_ref.shape[0], add, (zero, zero))
    own = jnp.where((energy_row >= 0) & (energy_lane >= 0), own, 0.0)
    side = jnp.where(energy_lane >= 0, side, 0.0)
    spread = jnp.where(energy_row == lanes, 1.0, 0.0)
    return own, side, spread


def spread_out(table, out_ref):
    height, width = out_ref.shape
    left_row = lax.broadcasted_iota(jnp.int32, (height, LANES), 0)
    left_lane = lax.broadcasted_iota(jnp.int32, (height, LANES), 1)
    left = jnp.where(left_row // TILE == left_lane, 1.0, 0.0).astype(jnp.bfloat16)
    right_row = lax.broadcasted_iota(jnp.int32, (LANES, width), 0)
    right_lane = lax.broadcasted_iota(jnp.int32, (LANES, width), 1)
    right = jnp.where(right_lane // TILE == right_row, 1.0, 0.0).astype(jnp.bfloat16)
    tall = jnp.dot(left, table.astype(jnp.bfloat16), preferred_element_type=jnp.float32)
    full = jnp.dot(tall.astype(jnp.bfloat16), right, preferred_element_type=jnp.float32)
    row = lax.broadcasted_iota(jnp.int32, (height, width), 0)
    lane = lax.broadcasted_iota(jnp.int32, (height, width), 1)
    out_ref[...] = jnp.where(row % TILE == lane % TILE, full, 0.0).astype(jnp.bfloat16)


def kernel(
    groups, blocks, light, counts_ref, shift_ref, weight_ref, r_ref, c_ref, o_ref,
    left, mixed, lesser, moved, own_mat, side_mat, spread_mat, side_part, below, above,
    sigma, back, total, send_f, recv_f, send_a, recv_a,
    send_b, recv_b, local_a, local_b,
    send_up, recv_up, send_dn, recv_dn,
):
    per_group, _, orbitals, _ = r_ref.shape
    slots = groups * per_group
    chunks = moved.shape[0]
    depth = groups * TILE
    me = lax.axis_index("energy")
    block = lax.axis_index("atoms")
    has_below = block > 0
    has_above = block < blocks - 1

    barrier = pltpu.get_barrier_semaphore()
    for d in range(1, groups):
        pl.semaphore_signal(barrier, inc=1, device_id={"energy": lax.rem(me + d, groups)}, device_id_type=MESH)

    @pl.when(has_below)
    def _():
        pl.semaphore_signal(barrier, inc=1, device_id={"atoms": block - 1}, device_id_type=MESH)

    @pl.when(has_above)
    def _():
        pl.semaphore_signal(barrier, inc=1, device_id={"atoms": block + 1}, device_id_type=MESH)

    @pl.when(jnp.logical_not(has_below))
    def _():
        below[...] = jnp.zeros_like(below)

    @pl.when(jnp.logical_not(has_above))
    def _():
        above[...] = jnp.zeros_like(above)

    for group in light:
        for q in range(chunks):
            moved[q, (group + 1) * per_group - 1] = jnp.zeros(moved.shape[2:], jnp.bfloat16)

    def is_light(group):
        flag = group < 0
        for one in light:
            flag = flag | (group == one)
        return flag

    def sized(group, act):
        if not light:
            act(per_group)
            return
        flag = is_light(group)
        pl.when(flag)(lambda: act(per_group - 1))
        pl.when(jnp.logical_not(flag))(lambda: act(per_group))

    if light:
        @pl.when(is_light(me))
        def _():
            back[per_group - 1] = jnp.zeros(back.shape[1:], jnp.bfloat16)

    def complex_rows(dst, s, rows, lower, real, imag):
        dst[s, rows, :orbitals] = real
        dst[s, rows, orbitals:] = -imag
        dst[s, lower, :orbitals] = imag
        dst[s, lower, orbitals:] = real

    def mix(s):
        def copy_rows(i, carry):
            at = pl.multiple_of(i * LANES, LANES)
            rows, lower = pl.ds(at, LANES), pl.ds(at + orbitals, LANES)
            complex_rows(left, s, rows, lower, r_ref[s, 0, rows, :], r_ref[s, 1, rows, :])
            return carry

        def mix_rows(i, carry):
            at = pl.multiple_of(i * LANES, LANES)
            rows, lower = pl.ds(at, LANES), pl.ds(at + orbitals, LANES)
            contact = c_ref[s].reshape(2 * orbitals, orbitals)
            real = jnp.dot(left[s, rows, :], contact, preferred_element_type=jnp.float32)
            imag = jnp.dot(left[s, lower, :], contact, preferred_element_type=jnp.float32)
            complex_rows(mixed, s, rows, lower, real.astype(jnp.bfloat16), imag.astype(jnp.bfloat16))
            return carry

        lax.fori_loop(0, orbitals // LANES, copy_rows, 0)
        lax.fori_loop(0, orbitals // LANES, mix_rows, 0)

    mix(0)

    neighbours = jnp.where(has_below, 1, 0) + jnp.where(has_above, 1, 0)
    pl.semaphore_wait(barrier, groups - 1 + neighbours)

    def tile_rows(q, peer):
        return pl.ds(pl.multiple_of((q * groups + peer) * TILE, TILE), TILE)

    def first_copy(q, d):
        peer = lax.rem(me + d, groups)
        return pltpu.make_async_remote_copy(
            src_ref=lesser.at[pl.ds(0, 1), tile_rows(q, peer), :],
            dst_ref=moved.at[q, pl.ds(me * per_group, 1)],
            send_sem=send_f.at[q, d], recv_sem=recv_f.at[q, d],
            device_id={"energy": peer}, device_id_type=MESH,
        )

    def out_copy(q, d, count):
        peer = lax.rem(me + d, groups)
        return pltpu.make_async_remote_copy(
            src_ref=lesser.at[pl.ds(1, count - 1), tile_rows(q, peer), :],
            dst_ref=moved.at[q, pl.ds(me * per_group + 1, count - 1)],
            send_sem=send_a.at[q, d], recv_sem=recv_a.at[q, d],
            device_id={"energy": peer}, device_id_type=MESH,
        )

    def out_local(q, count):
        return pltpu.make_async_copy(
            lesser.at[pl.ds(0, count), tile_rows(q, me), :],
            moved.at[q, pl.ds(me * per_group, count)],
            local_a.at[q],
        )

    def back_copy(q, d, count):
        peer = lax.rem(me + d, groups)
        return pltpu.make_async_remote_copy(
            src_ref=sigma.at[q, pl.ds(peer * per_group, count)],
            dst_ref=back.at[pl.ds(0, count), tile_rows(q, me), :],
            send_sem=send_b.at[q, d], recv_sem=recv_b.at[q, d],
            device_id={"energy": peer}, device_id_type=MESH,
        )

    def back_local(q, count):
        return pltpu.make_async_copy(
            sigma.at[q, pl.ds(me * per_group, count)],
            back.at[pl.ds(0, count), tile_rows(q, me), :],
            local_b.at[q],
        )

    def each_peer(act):
        def one(d, carry):
            act(d)
            return carry

        lax.fori_loop(1, groups, one, 0)

    def source(d):
        return lax.rem(me + groups - d, groups)

    def target(d):
        return lax.rem(me + d, groups)

    def up_copy(q):
        return pltpu.make_async_remote_copy(
            src_ref=side_part.at[q], dst_ref=below.at[q],
            send_sem=send_up.at[q], recv_sem=recv_up.at[q],
            device_id={"atoms": block + 1}, device_id_type=MESH,
        )

    def down_copy(q):
        return pltpu.make_async_remote_copy(
            src_ref=side_part.at[q], dst_ref=above.at[q],
            send_sem=send_dn.at[q], recv_sem=recv_dn.at[q],
            device_id={"atoms": block - 1}, device_id_type=MESH,
        )

    def lesser_rows(q, first, last):
        rows = pl.ds(pl.multiple_of(q * depth, depth), depth)

        def one(s, carry):
            lesser[s, rows, :] = lax.dot_general(
                mixed[s, rows, :], left[s, :orbitals, :], (((1,), (1,)), ((), ())),
                preferred_element_type=jnp.float32,
            ).astype(jnp.bfloat16)
            return carry

        lax.fori_loop(first, last, one, 0)

    def send_first(q, carry):
        lesser_rows(q, 0, 1)
        each_peer(lambda d: first_copy(q, d).start())
        return carry

    def send_rest(q, carry):
        lesser_rows(q, 1, per_group)
        sized(me, lambda n: each_peer(lambda d: out_copy(q, d, n).start()))
        sized(me, lambda n: out_local(q, n).start())
        return carry

    def send_both(q, carry):
        return send_rest(q, send_first(q, carry))

    early = min(2, chunks)
    lax.fori_loop(0, early, send_first, 0)

    def mix_later(s, carry):
        mix(s)
        return carry

    lax.fori_loop(1, per_group, mix_later, 0)
    lax.fori_loop(0, early, send_rest, 0)
    lax.fori_loop(early, chunks, send_both, 0)

    own, side, spread = coupling_tables(groups, per_group, counts_ref, shift_ref, weight_ref)
    spread_out(own, own_mat)
    spread_out(side, side_mat)
    spread_out(spread, spread_mat)

    def send_side(q):
        def got(d):
            first_copy(q, d).wait_recv()
            sized(source(d), lambda n: out_copy(q, d, n).wait_recv())

        each_peer(got)
        sized(me, lambda n: out_local(q, n).wait())
        values = moved[q].reshape(slots * TILE, orbitals)
        part = jnp.dot(side_mat[...], values, preferred_element_type=jnp.float32)
        side_part[q] = part.astype(jnp.bfloat16).reshape(side_part.shape[1:])

        @pl.when(has_above)
        def _():
            up_copy(q).start()

        @pl.when(has_below)
        def _():
            down_copy(q).start()

    def send_sigma(q):
        @pl.when(has_below)
        def _():
            up_copy(q).wait_recv()

        @pl.when(has_above)
        def _():
            down_copy(q).wait_recv()

        values = moved[q].reshape(slots * TILE, orbitals)
        flat = (side_mat.shape[0], orbitals)
        result = jnp.dot(own_mat[...], values, preferred_element_type=jnp.float32)
        result = result + jnp.dot(spread_mat[...], below[q].reshape(flat), preferred_element_type=jnp.float32)
        result = result + jnp.dot(spread_mat[...], above[q].reshape(flat), preferred_element_type=jnp.float32)
        sigma[q] = result.astype(jnp.bfloat16).reshape(sigma.shape[1:])
        each_peer(lambda d: sized(target(d), lambda n: back_copy(q, d, n).start()))
        sized(me, lambda n: back_local(q, n).start())

    send_side(0)

    def middle(q, carry):
        send_side(q)
        send_sigma(q - 1)
        return carry

    lax.fori_loop(1, chunks, middle, 0)
    send_sigma(chunks - 1)

    def arrive(q, carry):
        sized(me, lambda n: each_peer(lambda d: back_copy(q, d, n).wait_recv()))
        sized(me, lambda n: back_local(q, n).wait())
        return carry

    lax.fori_loop(0, chunks - 1, arrive, 0)
    cut = (chunks - 1) * depth

    row_blocks = 2 * orbitals // LANES

    def block_rows(i):
        return i // row_blocks, pl.ds(pl.multiple_of(lax.rem(i, row_blocks) * LANES, LANES), LANES)

    def head(i, carry):
        s, rows = block_rows(i)
        total[s, rows, :] = jnp.dot(left[s, rows, :cut], back[s, :cut, :], preferred_element_type=jnp.float32)
        return carry

    lax.fori_loop(0, per_group * row_blocks, head, 0)
    arrive(chunks - 1, 0)

    def tail(s, carry):
        last = jnp.dot(left[s, :, cut:], back[s, cut:, :], preferred_element_type=jnp.float32)
        o_ref[s] = (total[s] + last).astype(jnp.bfloat16).reshape(2, orbitals, orbitals)
        return carry

    lax.fori_loop(0, per_group, tail, 0)

    def drain(q, carry):
        def gone(d):
            first_copy(q, d).wait_send()
            sized(me, lambda n: out_copy(q, d, n).wait_send())
            sized(target(d), lambda n: back_copy(q, d, n).wait_send())

        each_peer(gone)

        @pl.when(has_above)
        def _():
            up_copy(q).wait_send()

        @pl.when(has_below)
        def _():
            down_copy(q).wait_send()

        return carry

    lax.fori_loop(0, chunks, drain, 0)


def exchange(groups, blocks, light, identity, retarded, contact, energy_counts, phonon_shift, phonon_weight):
    per_group, parts, orbitals, _ = retarded.shape
    slots = groups * per_group
    rows = parts * orbitals
    chunks = rows // (groups * TILE)
    energies = 2 * groups
    bf16, f32 = jnp.bfloat16, jnp.float32
    smem = pl.BlockSpec(memory_space=pltpu.SMEM)
    vmem = pl.BlockSpec(memory_space=pltpu.VMEM)
    dma = pltpu.SemaphoreType.DMA
    return pl.pallas_call(
        functools.partial(kernel, groups, blocks, light),
        out_shape=jax.ShapeDtypeStruct(retarded.shape, bf16),
        in_specs=[smem, smem, smem, vmem, vmem],
        out_specs=vmem,
        scratch_shapes=[
            pltpu.VMEM((per_group, rows, rows), bf16),
            pltpu.VMEM((per_group, rows, rows), bf16),
            pltpu.VMEM((per_group, rows, orbitals), bf16),
            pltpu.VMEM((chunks, slots, TILE, orbitals), bf16),
            pltpu.VMEM((slots * TILE, slots * TILE), bf16),
            pltpu.VMEM((energies * TILE, slots * TILE), bf16),
            pltpu.VMEM((slots * TILE, energies * TILE), bf16),
            pltpu.VMEM((chunks, energies, TILE, orbitals), bf16),
            pltpu.VMEM((chunks, energies, TILE, orbitals), bf16),
            pltpu.VMEM((chunks, energies, TILE, orbitals), bf16),
            pltpu.VMEM((chunks, slots, TILE, orbitals), bf16),
            pltpu.VMEM((per_group, rows, orbitals), bf16),
            pltpu.VMEM((per_group, rows, orbitals), f32),
            dma((chunks, groups)), dma((chunks, groups)), dma((chunks, groups)),
            dma((chunks, groups)), dma((chunks, groups)), dma((chunks, groups)),
            dma((chunks,)), dma((chunks,)),
            dma((chunks,)), dma((chunks,)), dma((chunks,)), dma((chunks,)),
        ],
        compiler_params=pltpu.CompilerParams(
            collective_id=identity, has_side_effects=True, vmem_limit_bytes=40 << 20
        ),
    )(energy_counts, phonon_shift, phonon_weight, retarded, contact)


LIGHT = False


def on_device(groups, blocks, retarded, contact, energy_counts, phonon_shift, phonon_weight):
    operands = (retarded[0], contact[0], energy_counts, phonon_shift, phonon_weight)
    if not LIGHT:
        return exchange(groups, blocks, (), 0, *operands)[None]
    pairs = groups // 2
    full = (energy_counts == retarded.shape[1]).reshape(pairs, 2).any(axis=1)
    chosen = jnp.argmin(full.astype(jnp.int32))
    branches = [
        functools.partial(exchange, groups, blocks, (2 * pair, 2 * pair + 1), pair) for pair in range(pairs)
    ]
    return lax.switch(chosen, branches, *operands)[None]


def solution(mesh):
    split = P("atoms", "energy", None, None, None)
    return jax.shard_map(
        functools.partial(on_device, mesh.shape["energy"], mesh.shape["atoms"]),
        mesh=mesh, in_specs=(split, split, P(), P(), P()), out_specs=split, check_vma=False,
    )
```

```python
import functools

import jax
import jax.numpy as jnp
from jax import lax
from jax.experimental import pallas as pl
from jax.experimental.pallas import tpu as pltpu
from jax.sharding import PartitionSpec as P

TILE = 16
LANES = 128
MESH = pl.DeviceIdType.MESH


def coupling_tables(groups, per_group, counts_ref, shift_ref, weight_ref):
    rows = lax.broadcasted_iota(jnp.int32, (LANES, LANES), 0)
    lanes = lax.broadcasted_iota(jnp.int32, (LANES, LANES), 1)

    def slot_energy(index):
        energy = jnp.full((LANES, LANES), -1, jnp.int32)
        start = jnp.int32(0)
        for group in range(groups):
            count = counts_ref[group]
            for s in range(per_group):
                here = (index == group * per_group + s) & (s < count)
                energy = jnp.where(here, start + s, energy)
            start = start + count
        return energy

    energy_row = slot_energy(rows)
    energy_lane = slot_energy(lanes)
    own_space = energy_lane - energy_row
    side_space = energy_lane - rows

    def add(m, sums):
        own, side = sums
        shift = shift_ref[m]
        own = own + jnp.where(own_space == shift, weight_ref[0, m], 0.0)
        own = own + jnp.where(own_space == -shift, weight_ref[1, m], 0.0)
        side = side + jnp.where(side_space == shift, weight_ref[2, m], 0.0)
        side = side + jnp.where(side_space == -shift, weight_ref[3, m], 0.0)
        return own, side

    zero = jnp.zeros((LANES, LANES), jnp.float32)
    own, side = lax.fori_loop(0, shift_ref.shape[0], add, (zero, zero))
    own = jnp.where((energy_row >= 0) & (energy_lane >= 0), own, 0.0)
    side = jnp.where(energy_lane >= 0, side, 0.0)
    spread = jnp.where(energy_row == lanes, 1.0, 0.0)
    return own, side, spread


def spread_out(table, out_ref):
    height, width = out_ref.shape
    left_row = lax.broadcasted_iota(jnp.int32, (height, LANES), 0)
    left_lane = lax.broadcasted_iota(jnp.int32, (height, LANES), 1)
    left = jnp.where(left_row // TILE == left_lane, 1.0, 0.0).astype(jnp.bfloat16)
    right_row = lax.broadcasted_iota(jnp.int32, (LANES, width), 0)
    right_lane = lax.broadcasted_iota(jnp.int32, (LANES, width), 1)
    right = jnp.where(right_lane // TILE == right_row, 1.0, 0.0).astype(jnp.bfloat16)
    tall = jnp.dot(left, table.astype(jnp.bfloat16), preferred_element_type=jnp.float32)
    full = jnp.dot(tall.astype(jnp.bfloat16), right, preferred_element_type=jnp.float32)
    row = lax.broadcasted_iota(jnp.int32, (height, width), 0)
    lane = lax.broadcasted_iota(jnp.int32, (height, width), 1)
    out_ref[...] = jnp.where(row % TILE == lane % TILE, full, 0.0).astype(jnp.bfloat16)


def kernel(
    groups, blocks, light, counts_ref, shift_ref, weight_ref, r_ref, c_ref, o_ref,
    left, mixed, lesser, moved, own_mat, side_mat, spread_mat, side_part, below, above,
    sigma, back, total, send_f, recv_f, send_a, recv_a,
    send_b, recv_b, local_a, local_b,
    send_up, recv_up, send_dn, recv_dn,
):
    per_group, _, orbitals, _ = r_ref.shape
    slots = groups * per_group
    chunks = moved.shape[0]
    depth = groups * TILE
    me = lax.axis_index("energy")
    block = lax.axis_index("atoms")
    has_below = block > 0
    has_above = block < blocks - 1

    barrier = pltpu.get_barrier_semaphore()
    for d in range(1, groups):
        pl.semaphore_signal(barrier, inc=1, device_id={"energy": lax.rem(me + d, groups)}, device_id_type=MESH)

    @pl.when(has_below)
    def _():
        pl.semaphore_signal(barrier, inc=1, device_id={"atoms": block - 1}, device_id_type=MESH)

    @pl.when(has_above)
    def _():
        pl.semaphore_signal(barrier, inc=1, device_id={"atoms": block + 1}, device_id_type=MESH)

    @pl.when(jnp.logical_not(has_below))
    def _():
        below[...] = jnp.zeros_like(below)

    @pl.when(jnp.logical_not(has_above))
    def _():
        above[...] = jnp.zeros_like(above)

    for group in light:
        for q in range(chunks):
            moved[q, (group + 1) * per_group - 1] = jnp.zeros(moved.shape[2:], jnp.bfloat16)

    def is_light(group):
        flag = group < 0
        for one in light:
            flag = flag | (group == one)
        return flag

    def sized(group, act):
        if not light:
            act(per_group)
            return
        flag = is_light(group)
        pl.when(flag)(lambda: act(per_group - 1))
        pl.when(jnp.logical_not(flag))(lambda: act(per_group))

    if light:
        @pl.when(is_light(me))
        def _():
            back[per_group - 1] = jnp.zeros(back.shape[1:], jnp.bfloat16)

    def complex_rows(dst, s, rows, lower, real, imag):
        dst[s, rows, :orbitals] = real
        dst[s, rows, orbitals:] = -imag
        dst[s, lower, :orbitals] = imag
        dst[s, lower, orbitals:] = real

    def mix(s):
        def copy_rows(i, carry):
            at = pl.multiple_of(i * LANES, LANES)
            rows, lower = pl.ds(at, LANES), pl.ds(at + orbitals, LANES)
            complex_rows(left, s, rows, lower, r_ref[s, 0, rows, :], r_ref[s, 1, rows, :])
            return carry

        def mix_rows(i, carry):
            at = pl.multiple_of(i * LANES, LANES)
            rows, lower = pl.ds(at, LANES), pl.ds(at + orbitals, LANES)
            contact = c_ref[s].reshape(2 * orbitals, orbitals)
            real = jnp.dot(left[s, rows, :], contact, preferred_element_type=jnp.float32)
            imag = jnp.dot(left[s, lower, :], contact, preferred_element_type=jnp.float32)
            complex_rows(mixed, s, rows, lower, real.astype(jnp.bfloat16), imag.astype(jnp.bfloat16))
            return carry

        lax.fori_loop(0, orbitals // LANES, copy_rows, 0)
        lax.fori_loop(0, orbitals // LANES, mix_rows, 0)

    mix(0)

    neighbours = jnp.where(has_below, 1, 0) + jnp.where(has_above, 1, 0)
    pl.semaphore_wait(barrier, groups - 1 + neighbours)

    def tile_rows(q, peer):
        return pl.ds(pl.multiple_of((q * groups + peer) * TILE, TILE), TILE)

    def first_copy(q, d):
        peer = lax.rem(me + d, groups)
        return pltpu.make_async_remote_copy(
            src_ref=lesser.at[pl.ds(0, 1), tile_rows(q, peer), :],
            dst_ref=moved.at[q, pl.ds(me * per_group, 1)],
            send_sem=send_f.at[q, d], recv_sem=recv_f.at[q, d],
            device_id={"energy": peer}, device_id_type=MESH,
        )

    def out_copy(q, d, count):
        peer = lax.rem(me + d, groups)
        return pltpu.make_async_remote_copy(
            src_ref=lesser.at[pl.ds(1, count - 1), tile_rows(q, peer), :],
            dst_ref=moved.at[q, pl.ds(me * per_group + 1, count - 1)],
            send_sem=send_a.at[q, d], recv_sem=recv_a.at[q, d],
            device_id={"energy": peer}, device_id_type=MESH,
        )

    def out_local(q, count):
        return pltpu.make_async_copy(
            lesser.at[pl.ds(0, count), tile_rows(q, me), :],
            moved.at[q, pl.ds(me * per_group, count)],
            local_a.at[q],
        )

    def back_copy(q, d, count):
        peer = lax.rem(me + d, groups)
        return pltpu.make_async_remote_copy(
            src_ref=sigma.at[q, pl.ds(peer * per_group, count)],
            dst_ref=back.at[pl.ds(0, count), tile_rows(q, me), :],
            send_sem=send_b.at[q, d], recv_sem=recv_b.at[q, d],
            device_id={"energy": peer}, device_id_type=MESH,
        )

    def back_local(q, count):
        return pltpu.make_async_copy(
            sigma.at[q, pl.ds(me * per_group, count)],
            back.at[pl.ds(0, count), tile_rows(q, me), :],
            local_b.at[q],
        )

    def each_peer(act):
        def one(d, carry):
            act(d)
            return carry

        lax.fori_loop(1, groups, one, 0)

    def source(d):
        return lax.rem(me + groups - d, groups)

    def target(d):
        return lax.rem(me + d, groups)

    def up_copy(q):
        return pltpu.make_async_remote_copy(
            src_ref=side_part.at[q], dst_ref=below.at[q],
            send_sem=send_up.at[q], recv_sem=recv_up.at[q],
            device_id={"atoms": block + 1}, device_id_type=MESH,
        )

    def down_copy(q):
        return pltpu.make_async_remote_copy(
            src_ref=side_part.at[q], dst_ref=above.at[q],
            send_sem=send_dn.at[q], recv_sem=recv_dn.at[q],
            device_id={"atoms": block - 1}, device_id_type=MESH,
        )

    def lesser_rows(q, first, last):
        rows = pl.ds(pl.multiple_of(q * depth, depth), depth)

        def one(s, carry):
            lesser[s, rows, :] = lax.dot_general(
                mixed[s, rows, :], left[s, :orbitals, :], (((1,), (1,)), ((), ())),
                preferred_element_type=jnp.float32,
            ).astype(jnp.bfloat16)
            return carry

        lax.fori_loop(first, last, one, 0)

    def send_first(q, carry):
        lesser_rows(q, 0, 1)
        each_peer(lambda d: first_copy(q, d).start())
        return carry

    def send_rest(q, carry):
        lesser_rows(q, 1, per_group)
        sized(me, lambda n: each_peer(lambda d: out_copy(q, d, n).start()))
        sized(me, lambda n: out_local(q, n).start())
        return carry

    def send_both(q, carry):
        return send_rest(q, send_first(q, carry))

    early = min(2, chunks)
    lax.fori_loop(0, early, send_first, 0)

    def mix_later(s, carry):
        mix(s)
        return carry

    lax.fori_loop(1, per_group, mix_later, 0)
    lax.fori_loop(0, early, send_rest, 0)
    lax.fori_loop(early, chunks, send_both, 0)

    own, side, spread = coupling_tables(groups, per_group, counts_ref, shift_ref, weight_ref)
    spread_out(own, own_mat)
    spread_out(side, side_mat)
    spread_out(spread, spread_mat)

    def send_side(q):
        def got(d):
            first_copy(q, d).wait_recv()
            sized(source(d), lambda n: out_copy(q, d, n).wait_recv())

        each_peer(got)
        sized(me, lambda n: out_local(q, n).wait())
        values = moved[q].reshape(slots * TILE, orbitals)
        part = jnp.dot(side_mat[...], values, preferred_element_type=jnp.float32)
        side_part[q] = part.astype(jnp.bfloat16).reshape(side_part.shape[1:])

        @pl.when(has_above)
        def _():
            up_copy(q).start()

        @pl.when(has_below)
        def _():
            down_copy(q).start()

    def send_sigma(q):
        @pl.when(has_below)
        def _():
            up_copy(q).wait_recv()

        @pl.when(has_above)
        def _():
            down_copy(q).wait_recv()

        values = moved[q].reshape(slots * TILE, orbitals)
        flat = (side_mat.shape[0], orbitals)
        result = jnp.dot(own_mat[...], values, preferred_element_type=jnp.float32)
        result = result + jnp.dot(spread_mat[...], below[q].reshape(flat), preferred_element_type=jnp.float32)
        result = result + jnp.dot(spread_mat[...], above[q].reshape(flat), preferred_element_type=jnp.float32)
        sigma[q] = result.astype(jnp.bfloat16).reshape(sigma.shape[1:])
        each_peer(lambda d: sized(target(d), lambda n: back_copy(q, d, n).start()))
        sized(me, lambda n: back_local(q, n).start())

    send_side(0)

    def middle(q, carry):
        send_side(q)
        send_sigma(q - 1)
        return carry

    lax.fori_loop(1, chunks, middle, 0)
    send_sigma(chunks - 1)

    def arrive(q, carry):
        sized(me, lambda n: each_peer(lambda d: back_copy(q, d, n).wait_recv()))
        sized(me, lambda n: back_local(q, n).wait())
        return carry

    lax.fori_loop(0, chunks - 1, arrive, 0)
    cut = (chunks - 1) * depth

    row_blocks = 2 * orbitals // LANES

    def block_rows(i):
        return i // row_blocks, pl.ds(pl.multiple_of(lax.rem(i, row_blocks) * LANES, LANES), LANES)

    def head(i, carry):
        s, rows = block_rows(i)
        total[s, rows, :] = jnp.dot(left[s, rows, :cut], back[s, :cut, :], preferred_element_type=jnp.float32)
        return carry

    lax.fori_loop(0, per_group * row_blocks, head, 0)
    arrive(chunks - 1, 0)

    def tail(s, carry):
        last = jnp.dot(left[s, :, cut:], back[s, cut:, :], preferred_element_type=jnp.float32)
        o_ref[s] = (total[s] + last).astype(jnp.bfloat16).reshape(2, orbitals, orbitals)
        return carry

    lax.fori_loop(0, per_group, tail, 0)

    def drain(q, carry):
        def gone(d):
            first_copy(q, d).wait_send()
            sized(me, lambda n: out_copy(q, d, n).wait_send())
            sized(target(d), lambda n: back_copy(q, d, n).wait_send())

        each_peer(gone)

        @pl.when(has_above)
        def _():
            up_copy(q).wait_send()

        @pl.when(has_below)
        def _():
            down_copy(q).wait_send()

        return carry

    lax.fori_loop(0, chunks, drain, 0)


def exchange(groups, blocks, light, identity, retarded, contact, energy_counts, phonon_shift, phonon_weight):
    per_group, parts, orbitals, _ = retarded.shape
    slots = groups * per_group
    rows = parts * orbitals
    chunks = rows // (groups * TILE)
    energies = 2 * groups
    bf16, f32 = jnp.bfloat16, jnp.float32
    smem = pl.BlockSpec(memory_space=pltpu.SMEM)
    vmem = pl.BlockSpec(memory_space=pltpu.VMEM)
    dma = pltpu.SemaphoreType.DMA
    return pl.pallas_call(
        functools.partial(kernel, groups, blocks, light),
        out_shape=jax.ShapeDtypeStruct(retarded.shape, bf16),
        in_specs=[smem, smem, smem, vmem, vmem],
        out_specs=vmem,
        scratch_shapes=[
            pltpu.VMEM((per_group, rows, rows), bf16),
            pltpu.VMEM((per_group, rows, rows), bf16),
            pltpu.VMEM((per_group, rows, orbitals), bf16),
            pltpu.VMEM((chunks, slots, TILE, orbitals), bf16),
            pltpu.VMEM((slots * TILE, slots * TILE), bf16),
            pltpu.VMEM((energies * TILE, slots * TILE), bf16),
            pltpu.VMEM((slots * TILE, energies * TILE), bf16),
            pltpu.VMEM((chunks, energies, TILE, orbitals), bf16),
            pltpu.VMEM((chunks, energies, TILE, orbitals), bf16),
            pltpu.VMEM((chunks, energies, TILE, orbitals), bf16),
            pltpu.VMEM((chunks, slots, TILE, orbitals), bf16),
            pltpu.VMEM((per_group, rows, orbitals), bf16),
            pltpu.VMEM((per_group, rows, orbitals), f32),
            dma((chunks, groups)), dma((chunks, groups)), dma((chunks, groups)),
            dma((chunks, groups)), dma((chunks, groups)), dma((chunks, groups)),
            dma((chunks,)), dma((chunks,)),
            dma((chunks,)), dma((chunks,)), dma((chunks,)), dma((chunks,)),
        ],
        compiler_params=pltpu.CompilerParams(
            collective_id=identity, has_side_effects=True, vmem_limit_bytes=40 << 20
        ),
    )(energy_counts, phonon_shift, phonon_weight, retarded, contact)


LIGHT = True


def on_device(groups, blocks, retarded, contact, energy_counts, phonon_shift, phonon_weight):
    operands = (retarded[0], contact[0], energy_counts, phonon_shift, phonon_weight)
    if not LIGHT:
        return exchange(groups, blocks, (), 0, *operands)[None]
    pairs = groups // 2
    full = (energy_counts == retarded.shape[1]).reshape(pairs, 2).any(axis=1)
    chosen = jnp.argmin(full.astype(jnp.int32))
    branches = [
        functools.partial(exchange, groups, blocks, (2 * pair, 2 * pair + 1), pair) for pair in range(pairs)
    ]
    return lax.switch(chosen, branches, *operands)[None]


def solution(mesh):
    split = P("atoms", "energy", None, None, None)
    return jax.shard_map(
        functools.partial(on_device, mesh.shape["energy"], mesh.shape["atoms"]),
        mesh=mesh, in_specs=(split, split, P(), P(), P()), out_specs=split, check_vma=False,
    )
```

```python
import functools
import itertools

import jax
import jax.numpy as jnp
import numpy as np
from jax import lax
from jax.experimental import pallas as pl
from jax.experimental.pallas import tpu as pltpu
from jax.sharding import PartitionSpec as P

TILE = 16
LANES = 128
LIGHT = 3
MESH = pl.DeviceIdType.MESH


def coupling_tables(groups, per_group, counts_ref, shift_ref, weight_ref):
    rows = lax.broadcasted_iota(jnp.int32, (LANES, LANES), 0)
    lanes = lax.broadcasted_iota(jnp.int32, (LANES, LANES), 1)

    def slot_energy(index):
        energy = jnp.full((LANES, LANES), -1, jnp.int32)
        start = jnp.int32(0)
        for group in range(groups):
            count = counts_ref[group]
            for s in range(per_group):
                here = (index == group * per_group + s) & (s < count)
                energy = jnp.where(here, start + s, energy)
            start = start + count
        return energy

    energy_row = slot_energy(rows)
    energy_lane = slot_energy(lanes)
    own_space = energy_lane - energy_row
    side_space = energy_lane - rows

    def add(m, sums):
        own, side = sums
        shift = shift_ref[m]
        own = own + jnp.where(own_space == shift, weight_ref[0, m], 0.0)
        own = own + jnp.where(own_space == -shift, weight_ref[1, m], 0.0)
        side = side + jnp.where(side_space == shift, weight_ref[2, m], 0.0)
        side = side + jnp.where(side_space == -shift, weight_ref[3, m], 0.0)
        return own, side

    zero = jnp.zeros((LANES, LANES), jnp.float32)
    own, side = lax.fori_loop(0, shift_ref.shape[0], add, (zero, zero))
    own = jnp.where((energy_row >= 0) & (energy_lane >= 0), own, 0.0)
    side = jnp.where(energy_lane >= 0, side, 0.0)
    spread = jnp.where(energy_row == lanes, 1.0, 0.0)
    return own, side, spread


def spread_out(table, out_ref):
    height, width = out_ref.shape
    right_row = lax.broadcasted_iota(jnp.int32, (LANES, width), 0)
    right_lane = lax.broadcasted_iota(jnp.int32, (LANES, width), 1)
    right = jnp.where(right_lane // TILE == right_row, 1.0, 0.0).astype(jnp.bfloat16)
    wide = jnp.dot(table.astype(jnp.bfloat16), right, preferred_element_type=jnp.float32).astype(jnp.bfloat16)

    def some_rows(i, carry):
        at = pl.multiple_of(i * LANES, LANES)
        left_row = lax.broadcasted_iota(jnp.int32, (LANES, LANES), 0) + at
        left_lane = lax.broadcasted_iota(jnp.int32, (LANES, LANES), 1)
        left = jnp.where(left_row // TILE == left_lane, 1.0, 0.0).astype(jnp.bfloat16)
        full = jnp.dot(left, wide, preferred_element_type=jnp.float32)
        out_ref[pl.ds(at, LANES), :] = jnp.where(
            right_row % TILE == right_lane % TILE, full, 0.0
        ).astype(jnp.bfloat16)
        return carry

    lax.fori_loop(0, height // LANES, some_rows, 0)


def kernel(
    groups, blocks, light, counts_ref, shift_ref, weight_ref, r_hbm, c_hbm, o_ref,
    r_ref, c_ref, load_r, load_c,
    left, mixed, lesser, moved, own_mat, side_mat, spread_mat, side_part, below, above,
    sigma, back, total, send_f, recv_f, send_a, recv_a,
    send_b, recv_b, local_a, local_b,
    send_up, recv_up, send_dn, recv_dn,
):
    per_group, _, orbitals, _ = r_hbm.shape
    slots = groups * per_group
    chunks = moved.shape[0]
    depth = groups * TILE
    me = lax.axis_index("energy")
    block = lax.axis_index("atoms")
    has_below = block > 0
    has_above = block < blocks - 1

    def load(s):
        return (
            pltpu.make_async_copy(r_hbm.at[s], r_ref.at[s], load_r.at[s]),
            pltpu.make_async_copy(c_hbm.at[s], c_ref.at[s], load_c.at[s]),
        )

    for s in range(per_group):
        for copy in load(s):
            copy.start()

    barrier = pltpu.get_barrier_semaphore()
    for d in range(1, groups):
        pl.semaphore_signal(barrier, inc=1, device_id={"energy": lax.rem(me + d, groups)}, device_id_type=MESH)

    @pl.when(has_below)
    def _():
        pl.semaphore_signal(barrier, inc=1, device_id={"atoms": block - 1}, device_id_type=MESH)

    @pl.when(has_above)
    def _():
        pl.semaphore_signal(barrier, inc=1, device_id={"atoms": block + 1}, device_id_type=MESH)

    @pl.when(jnp.logical_not(has_below))
    def _():
        below[...] = jnp.zeros_like(below)

    @pl.when(jnp.logical_not(has_above))
    def _():
        above[...] = jnp.zeros_like(above)

    for group in light:
        for q in range(chunks):
            moved[q, (group + 1) * per_group - 1] = jnp.zeros(moved.shape[2:], jnp.bfloat16)

    def is_light(group):
        flag = group < 0
        for one in light:
            flag = flag | (group == one)
        return flag

    def sized(group, act):
        if not light:
            act(per_group)
            return
        flag = is_light(group)
        pl.when(flag)(lambda: act(per_group - 1))
        pl.when(jnp.logical_not(flag))(lambda: act(per_group))

    if light:
        @pl.when(is_light(me))
        def _():
            back[per_group - 1] = jnp.zeros(back.shape[1:], jnp.bfloat16)

    def complex_rows(dst, s, rows, lower, real, imag):
        dst[s, rows, :orbitals] = real
        dst[s, rows, orbitals:] = -imag
        dst[s, lower, :orbitals] = imag
        dst[s, lower, orbitals:] = real

    def mix(s):
        def copy_rows(i, carry):
            at = pl.multiple_of(i * LANES, LANES)
            rows, lower = pl.ds(at, LANES), pl.ds(at + orbitals, LANES)
            complex_rows(left, s, rows, lower, r_ref[s, 0, rows, :], r_ref[s, 1, rows, :])
            return carry

        def mix_rows(i, carry):
            at = pl.multiple_of(i * LANES, LANES)
            rows, lower = pl.ds(at, LANES), pl.ds(at + orbitals, LANES)
            contact = c_ref[s].reshape(2 * orbitals, orbitals)
            real = jnp.dot(left[s, rows, :], contact, preferred_element_type=jnp.float32)
            imag = jnp.dot(left[s, lower, :], contact, preferred_element_type=jnp.float32)
            complex_rows(mixed, s, rows, lower, real.astype(jnp.bfloat16), imag.astype(jnp.bfloat16))
            return carry

        for copy in load(s):
            copy.wait()
        lax.fori_loop(0, orbitals // LANES, copy_rows, 0)
        lax.fori_loop(0, orbitals // LANES, mix_rows, 0)

    mix(0)

    neighbours = jnp.where(has_below, 1, 0) + jnp.where(has_above, 1, 0)
    pl.semaphore_wait(barrier, groups - 1 + neighbours)

    def tile_rows(q, peer):
        return pl.ds(pl.multiple_of((q * groups + peer) * TILE, TILE), TILE)

    def first_copy(q, d):
        peer = lax.rem(me + d, groups)
        return pltpu.make_async_remote_copy(
            src_ref=lesser.at[pl.ds(0, 1), tile_rows(q, peer), :],
            dst_ref=moved.at[q, pl.ds(me * per_group, 1)],
            send_sem=send_f.at[q, d], recv_sem=recv_f.at[q, d],
            device_id={"energy": peer}, device_id_type=MESH,
        )

    def out_copy(q, d, count):
        peer = lax.rem(me + d, groups)
        return pltpu.make_async_remote_copy(
            src_ref=lesser.at[pl.ds(1, count - 1), tile_rows(q, peer), :],
            dst_ref=moved.at[q, pl.ds(me * per_group + 1, count - 1)],
            send_sem=send_a.at[q, d], recv_sem=recv_a.at[q, d],
            device_id={"energy": peer}, device_id_type=MESH,
        )

    def out_local(q, count):
        return pltpu.make_async_copy(
            lesser.at[pl.ds(0, count), tile_rows(q, me), :],
            moved.at[q, pl.ds(me * per_group, count)],
            local_a.at[q],
        )

    def back_copy(q, d, count):
        peer = lax.rem(me + d, groups)
        return pltpu.make_async_remote_copy(
            src_ref=sigma.at[q, pl.ds(peer * per_group, count)],
            dst_ref=back.at[pl.ds(0, count), tile_rows(q, me), :],
            send_sem=send_b.at[q, d], recv_sem=recv_b.at[q, d],
            device_id={"energy": peer}, device_id_type=MESH,
        )

    def back_local(q, count):
        return pltpu.make_async_copy(
            sigma.at[q, pl.ds(me * per_group, count)],
            back.at[pl.ds(0, count), tile_rows(q, me), :],
            local_b.at[q],
        )

    def each_peer(act):
        def one(d, carry):
            act(d)
            return carry

        lax.fori_loop(1, groups, one, 0)

    def source(d):
        return lax.rem(me + groups - d, groups)

    def target(d):
        return lax.rem(me + d, groups)

    def up_copy(q):
        return pltpu.make_async_remote_copy(
            src_ref=side_part.at[q], dst_ref=below.at[q],
            send_sem=send_up.at[q], recv_sem=recv_up.at[q],
            device_id={"atoms": block + 1}, device_id_type=MESH,
        )

    def down_copy(q):
        return pltpu.make_async_remote_copy(
            src_ref=side_part.at[q], dst_ref=above.at[q],
            send_sem=send_dn.at[q], recv_sem=recv_dn.at[q],
            device_id={"atoms": block - 1}, device_id_type=MESH,
        )

    def lesser_rows(q, first, last):
        rows = pl.ds(pl.multiple_of(q * depth, depth), depth)

        def one(s, carry):
            lesser[s, rows, :] = lax.dot_general(
                mixed[s, rows, :], left[s, :orbitals, :], (((1,), (1,)), ((), ())),
                preferred_element_type=jnp.float32,
            ).astype(jnp.bfloat16)
            return carry

        lax.fori_loop(first, last, one, 0)

    def send_first(q, carry):
        lesser_rows(q, 0, 1)
        each_peer(lambda d: first_copy(q, d).start())
        return carry

    def send_rest(q, carry):
        lesser_rows(q, 1, per_group)
        sized(me, lambda n: each_peer(lambda d: out_copy(q, d, n).start()))
        sized(me, lambda n: out_local(q, n).start())
        return carry

    def send_later(q, carry):
        @pl.when(q >= early)
        def _():
            send_first(q, 0)

        return send_rest(q, carry)

    early = min(2, chunks)
    lax.fori_loop(0, early, send_first, 0)

    def mix_later(s, carry):
        mix(s)
        return carry

    lax.fori_loop(1, per_group, mix_later, 0)
    lax.fori_loop(0, chunks, send_later, 0)

    own, side, spread = coupling_tables(groups, per_group, counts_ref, shift_ref, weight_ref)
    spread_out(own, own_mat)
    spread_out(side, side_mat)
    spread_out(spread, spread_mat)

    def send_side(q):
        def got(d):
            first_copy(q, d).wait_recv()
            sized(source(d), lambda n: out_copy(q, d, n).wait_recv())

        each_peer(got)
        sized(me, lambda n: out_local(q, n).wait())
        def some_rows(i, carry):
            rows = pl.ds(pl.multiple_of(i * LANES, LANES), LANES)
            values = moved[q].reshape(slots * TILE, orbitals)
            part = jnp.dot(side_mat[rows, :], values, preferred_element_type=jnp.float32)
            tiles = pl.ds(i * (LANES // TILE), LANES // TILE)
            side_part[q, tiles] = part.astype(jnp.bfloat16).reshape(LANES // TILE, TILE, orbitals)
            return carry

        lax.fori_loop(0, side_mat.shape[0] // LANES, some_rows, 0)

        @pl.when(has_above)
        def _():
            up_copy(q).start()

        @pl.when(has_below)
        def _():
            down_copy(q).start()

    def send_sigma(q):
        @pl.when(has_below)
        def _():
            up_copy(q).wait_recv()

        @pl.when(has_above)
        def _():
            down_copy(q).wait_recv()

        flat = (side_mat.shape[0], orbitals)

        def some_rows(i, carry):
            rows = pl.ds(pl.multiple_of(i * LANES, LANES), LANES)
            values = moved[q].reshape(slots * TILE, orbitals)
            result = jnp.dot(own_mat[rows, :], values, preferred_element_type=jnp.float32)
            spread = spread_mat[rows, :]
            result = result + jnp.dot(spread, below[q].reshape(flat), preferred_element_type=jnp.float32)
            result = result + jnp.dot(spread, above[q].reshape(flat), preferred_element_type=jnp.float32)
            tiles = pl.ds(i * (LANES // TILE), LANES // TILE)
            sigma[q, tiles] = result.astype(jnp.bfloat16).reshape(LANES // TILE, TILE, orbitals)
            return carry

        lax.fori_loop(0, own_mat.shape[0] // LANES, some_rows, 0)
        each_peer(lambda d: sized(target(d), lambda n: back_copy(q, d, n).start()))
        sized(me, lambda n: back_local(q, n).start())

    def middle(q, carry):
        @pl.when(q < chunks)
        def _():
            send_side(q)

        @pl.when(q > 0)
        def _():
            send_sigma(q - 1)

        return carry

    lax.fori_loop(0, chunks + 1, middle, 0)

    def arrive(q, carry):
        sized(me, lambda n: each_peer(lambda d: back_copy(q, d, n).wait_recv()))
        sized(me, lambda n: back_local(q, n).wait())
        return carry

    lax.fori_loop(0, chunks - 1, arrive, 0)
    cut = (chunks - 1) * depth

    row_blocks = 2 * orbitals // LANES

    def block_rows(i):
        return i // row_blocks, pl.ds(pl.multiple_of(lax.rem(i, row_blocks) * LANES, LANES), LANES)

    def head(i, carry):
        s, rows = block_rows(i)
        total[s, rows, :] = jnp.dot(left[s, rows, :cut], back[s, :cut, :], preferred_element_type=jnp.float32)
        return carry

    lax.fori_loop(0, per_group * row_blocks, head, 0)
    arrive(chunks - 1, 0)

    def tail(s, carry):
        last = jnp.dot(left[s, :, cut:], back[s, cut:, :], preferred_element_type=jnp.float32)
        o_ref[s] = (total[s] + last).astype(jnp.bfloat16).reshape(2, orbitals, orbitals)
        return carry

    lax.fori_loop(0, per_group, tail, 0)

    def drain(q, carry):
        def gone(d):
            first_copy(q, d).wait_send()
            sized(me, lambda n: out_copy(q, d, n).wait_send())
            sized(target(d), lambda n: back_copy(q, d, n).wait_send())

        each_peer(gone)

        @pl.when(has_above)
        def _():
            up_copy(q).wait_send()

        @pl.when(has_below)
        def _():
            down_copy(q).wait_send()

        return carry

    lax.fori_loop(0, chunks, drain, 0)


def exchange(groups, blocks, light, identity, retarded, contact, energy_counts, phonon_shift, phonon_weight):
    per_group, parts, orbitals, _ = retarded.shape
    slots = groups * per_group
    rows = parts * orbitals
    chunks = rows // (groups * TILE)
    energies = 2 * groups
    bf16, f32 = jnp.bfloat16, jnp.float32
    smem = pl.BlockSpec(memory_space=pltpu.SMEM)
    vmem = pl.BlockSpec(memory_space=pltpu.VMEM)
    hbm = pl.BlockSpec(memory_space=pl.ANY)
    dma = pltpu.SemaphoreType.DMA
    return pl.pallas_call(
        functools.partial(kernel, groups, blocks, light),
        out_shape=jax.ShapeDtypeStruct(retarded.shape, bf16),
        in_specs=[smem, smem, smem, hbm, hbm],
        out_specs=vmem,
        scratch_shapes=[
            pltpu.VMEM(retarded.shape, bf16),
            pltpu.VMEM(retarded.shape, bf16),
            dma((per_group,)), dma((per_group,)),
            pltpu.VMEM((per_group, rows, rows), bf16),
            pltpu.VMEM((per_group, rows, rows), bf16),
            pltpu.VMEM((per_group, rows, orbitals), bf16),
            pltpu.VMEM((chunks, slots, TILE, orbitals), bf16),
            pltpu.VMEM((slots * TILE, slots * TILE), bf16),
            pltpu.VMEM((energies * TILE, slots * TILE), bf16),
            pltpu.VMEM((slots * TILE, energies * TILE), bf16),
            pltpu.VMEM((chunks, energies, TILE, orbitals), bf16),
            pltpu.VMEM((chunks, energies, TILE, orbitals), bf16),
            pltpu.VMEM((chunks, energies, TILE, orbitals), bf16),
            pltpu.VMEM((chunks, slots, TILE, orbitals), bf16),
            pltpu.VMEM((per_group, rows, orbitals), bf16),
            pltpu.VMEM((per_group, rows, orbitals), f32),
            dma((chunks, groups)), dma((chunks, groups)), dma((chunks, groups)),
            dma((chunks, groups)), dma((chunks, groups)), dma((chunks, groups)),
            dma((chunks,)), dma((chunks,)),
            dma((chunks,)), dma((chunks,)), dma((chunks,)), dma((chunks,)),
        ],
        compiler_params=pltpu.CompilerParams(
            collective_id=identity, has_side_effects=True, vmem_limit_bytes=58 << 20
        ),
    )(energy_counts, phonon_shift, phonon_weight, retarded, contact)


def light_sets(groups):
    if groups > 8:
        return [(group, group + 1) for group in range(0, groups, 2)]
    left = set(itertools.combinations(range(groups), (groups - 1) // 2))
    options = list(itertools.combinations(range(groups), LIGHT))
    family = []
    while left:
        best = max(options, key=lambda option: sum(not set(option) & set(full) for full in left))
        family.append(best)
        left = {full for full in left if set(best) & set(full)}
    return family


def on_device(groups, blocks, retarded, contact, energy_counts, phonon_shift, phonon_weight):
    operands = (retarded[0], contact[0], energy_counts, phonon_shift, phonon_weight)
    family = light_sets(groups)
    member = np.array([[group in one for group in range(groups)] for one in family], np.float32)
    full = (energy_counts == retarded.shape[1]).astype(jnp.float32)
    clashes = jnp.sum(member * full[None, :], axis=1)
    chosen = jnp.argmin(clashes)
    branches = [
        functools.partial(exchange, groups, blocks, one, identity) for identity, one in enumerate(family)
    ]
    return lax.switch(chosen, branches, *operands)[None]


def solution(mesh):
    split = P("atoms", "energy", None, None, None)
    return jax.shard_map(
        functools.partial(on_device, mesh.shape["energy"], mesh.shape["atoms"]),
        mesh=mesh, in_specs=(split, split, P(), P(), P()), out_specs=split, check_vma=False,
    )
```
